512 devices in a mesh: dp: 64 (over y, x, core), tensor: 8 (over z).
Axes of the slice: x: 4, y: 8, z: 8, core: 2. Of those that a mesh axis runs over, the one named last changes fastest.
Arguments:
- hidden_act: bfloat16 [32768, 1408], P('dp', 'tensor'), may hold values from -6 to 6
- cotangent: bfloat16 [32768, 2048], P('dp', 'tensor'), may hold values from -4 to 4
- down_table: bfloat16 [1408, 64, 2048], P('tensor', 'dp'), may hold values from -0.15625 to 0.15625
- expert_ids: int32 [128, 4], P('dp'), may hold values from 0 to 31, as said below
- merge_weights: float32 [128, 4], P('dp'), may hold values from 0.1 to 1
- owner_slot: int32 [32], replicated, may hold values from 0 to 63, as said below
Outputs:
- layer_out: bfloat16 [32768, 2048], P('dp', 'tensor')
- grad_hidden: bfloat16 [32768, 1408], P('dp', 'tensor')
- expert_grad: float32 [1408, 64, 2048], P('tensor', 'dp')
The draws below stay inside these ranges and needn't reach their ends.
Inputs may be any that keep to these rules, and one draw needn't show every extreme that they name: `expert_ids`: each segment lists 4 different experts; the 2 segments of one index of dp list exactly 6 different experts together. `owner_slot`: different experts have different slots; slot 63 always holds an expert.
All inputs are finite; a program needn't handle non-finite values.
Results may differ from the reference program's by a relative error of at most 0.013.
Values may be sent and summed in bfloat16 or wider, within the bound.
A program may use at most 128 MiB of HBM per device.

```python
import math
import jax
import jax.numpy as jnp
from jax import lax

D = 2048
FF = 1408
E = 32
K = 4
SEG = 256
POOL = 6
SEG_DEV = 2
SEGMENTS = 128
TOKENS = 32768
SLOTS = 64
N_DP = 64
N_TENSOR = 8


def draw_expert_ids(key, part):
    blocks = SEGMENTS // SEG_DEV

    def one_block(block_key):
        pool_ids = jax.random.permutation(jax.random.fold_in(block_key, 1), E)[:POOL]

        def one_segment(index):
            seg_key = jax.random.fold_in(block_key, 100 + index)
            picked = jax.random.permutation(seg_key, POOL)[:K]
            leading = jnp.arange(K)
            second = POOL - K + jnp.arange(K)
            chosen = jnp.where(index == 0, leading, jnp.where(index == 1, second, picked))
            shuffle = jax.random.permutation(jax.random.fold_in(seg_key, 7), K)
            return pool_ids[chosen[shuffle]]
        return jax.vmap(one_segment)(jnp.arange(SEG_DEV))
    block_keys = jax.vmap(lambda number: jax.random.fold_in(key, number))(jnp.arange(blocks))
    return jax.vmap(one_block)(block_keys).reshape(SEGMENTS, K).astype(jnp.int32)


def draw_owner_slot(key, part):
    slot_list = jax.random.permutation(jax.random.fold_in(key, 3), SLOTS)[:E]
    highest = jnp.max(slot_list)
    return jnp.where(slot_list == highest, SLOTS - 1, slot_list).astype(jnp.int32)


def block_scale(rng, dims, pieces, smallest, largest):
    def one(position, blocks):
        draws = jax.random.uniform(jax.random.fold_in(jax.random.fold_in(rng, 6), position), (blocks,), jnp.float32, smallest / len(pieces), largest / len(pieces))
        return jnp.repeat(jnp.exp(draws), dims[position] // blocks).reshape((-1,) + (1,) * (len(dims) - position - 1))

    level = one(*pieces[0])
    for cut in pieces[1:]:
        level = level * one(*cut)
    return level


def bell_draw(stream_key, extent, spread, bound, cuts=(), held_as=jnp.bfloat16):
    level = block_scale(stream_key, extent, cuts, -0.22, 0.18) if cuts else 1.0
    result = jax.random.normal(stream_key, extent, jnp.float32) * spread * level
    return jnp.minimum(jnp.maximum(result, -bound), bound).astype(held_as)


def setup_inputs(seed: int = 0) -> dict:
    seeds = jax.random.split(jax.random.key(seed), 7)
    hidden_act = bell_draw(seeds[0], (TOKENS, FF), 1.0, 6.0, ((0, 64), (1, 8)))
    cotangent = bell_draw(seeds[1], (TOKENS, D), 0.25, 4.0, ((0, 64), (1, 8)))
    down_table = bell_draw(seeds[2], (FF, SLOTS, D), FF ** -0.5, 0.15625, ((0, 8), (1, 64)))
    expert_ids = draw_expert_ids(jax.random.fold_in(seeds[6], 71), 0)
    merge_weights = jnp.clip(jnp.exp(math.log(1.0) - 2.3025851 * jax.random.uniform(seeds[4], (SEGMENTS, K), jnp.float32) ** block_scale(seeds[4], (SEGMENTS, K), ((0, 64),), -0.2, 0.2)), 0.1, 1.0)
    owner_slot = draw_owner_slot(jax.random.fold_in(seeds[6], 71), 0)
    return dict(hidden_act=hidden_act, cotangent=cotangent, down_table=down_table, expert_ids=expert_ids, merge_weights=merge_weights, owner_slot=owner_slot)


def reference(hidden_act, cotangent, down_table, expert_ids, merge_weights, owner_slot):
    ff_block = FF // N_TENSOR
    hidden_seg = hidden_act.reshape(N_DP, SEG_DEV, SEG, FF)
    cot_seg = cotangent.reshape(N_DP, SEG_DEV, SEG, D)
    slot_ids = owner_slot[expert_ids].astype(jnp.int32).reshape(N_DP, SEG_DEV, K)
    weight_groups = merge_weights.reshape(N_DP, SEG_DEV, K)
    id_groups = expert_ids.reshape(N_DP, SEG_DEV, K)

    def segment(totals, inputs):
        hidden_rows, cot_rows, slot_row, weight_row, id_row = inputs
        panel_set = jnp.take(down_table, slot_row, axis=1).astype(jnp.float32)
        merged = jnp.einsum("k,fkd->fd", weight_row, panel_set, precision=lax.Precision.HIGHEST).astype(jnp.bfloat16)
        block_terms = jnp.einsum(
            "tgf,gfd->gtd",
            hidden_rows.reshape(SEG, N_TENSOR, ff_block).astype(jnp.float32),
            merged.reshape(N_TENSOR, ff_block, D).astype(jnp.float32),
            precision=lax.Precision.HIGHEST,
        )
        rounded = lax.optimization_barrier(block_terms.astype(jnp.bfloat16))
        outputs = jnp.sum(rounded.astype(jnp.float32), axis=0).astype(jnp.bfloat16)
        grad_rows = jnp.dot(cot_rows, merged.T, preferred_element_type=jnp.float32).astype(jnp.bfloat16)
        seg_grad = jnp.dot(hidden_rows.T, cot_rows, preferred_element_type=jnp.float32).astype(jnp.bfloat16)
        update = weight_row[None, :, None] * seg_grad.astype(jnp.float32)[:, None, :]
        totals = totals.at[:, id_row, :].add(update)
        return totals, (outputs, grad_rows)

    def group(totals, inputs):
        start = jnp.zeros((FF, E, D), jnp.float32)
        group_totals, outs = lax.scan(segment, start, inputs)
        pooled = lax.optimization_barrier(group_totals.astype(jnp.bfloat16))
        return totals + pooled.astype(jnp.float32), outs

    begin = jnp.zeros((FF, E, D), jnp.float32)
    totals, (outputs, grad_rows) = lax.scan(group, begin, (hidden_seg, cot_seg, slot_ids, weight_groups, id_groups))
    expert_grad = jnp.zeros((FF, SLOTS, D), jnp.float32).at[:, owner_slot, :].set(totals)
    return outputs.reshape(TOKENS, D), grad_rows.reshape(TOKENS, FF), expert_grad
```

```python
import jax
import jax.numpy as jnp
from jax import lax
from jax.sharding import PartitionSpec as P

E = 32
K = 4
ROW_PARTS = 4
PAD = 4


def two_pieces(values):
    high = lax.reduce_precision(values, 8, 7)
    low = lax.reduce_precision(values - high, 8, 7)
    return high, low


def exchange(blocks):
    return lax.all_to_all(blocks, "dp", split_axis=0, concat_axis=0, tiled=True)


def split_panels(panels, count):
    lead, ff_local, width = panels.shape
    cols = count // ROW_PARTS
    view = panels.reshape(lead, ROW_PARTS, ff_local // ROW_PARTS, cols, width // cols)
    return jnp.transpose(view, (1, 3, 0, 2, 4)).reshape(
        count, lead, ff_local // ROW_PARTS, width // cols
    )


def join_panels(chunks):
    count, lead, rows, lanes = chunks.shape
    cols = count // ROW_PARTS
    view = chunks.reshape(ROW_PARTS, cols, lead, rows, lanes)
    return jnp.transpose(view, (2, 0, 3, 1, 4)).reshape(lead, ROW_PARTS * rows, cols * lanes)


def body(hidden_act, cotangent, down_table, expert_ids, merge_weights, owner_slot):
    count = lax.axis_size("dp")
    seg_count = expert_ids.shape[0]
    ff_local, _, width = down_table.shape
    row_count = hidden_act.shape[0]
    seg_len = row_count // seg_count
    rows = ff_local // ROW_PARTS
    lanes = width * ROW_PARTS // count
    listed = seg_count * K

    full_cot = lax.all_gather(cotangent, "tensor", axis=1, tiled=True)

    high, low = two_pieces(merge_weights)
    meta = jnp.concatenate(
        [expert_ids.astype(jnp.float32).reshape(-1), high.reshape(-1), low.reshape(-1)]
    ).astype(jnp.bfloat16)
    meta = jnp.pad(meta[None, :], ((0, PAD - 1), (0, lanes - 3 * listed)))
    table_chunks = split_panels(jnp.transpose(down_table, (1, 0, 2)), count)[:, 0]
    outgoing = jnp.concatenate(
        [table_chunks, jnp.broadcast_to(meta[None], (count, PAD, lanes))], axis=1
    )
    arrived = exchange(outgoing)
    by_slot = arrived[:, :rows]
    meta_all = arrived[:, rows, : 3 * listed].astype(jnp.float32)
    ids_all = meta_all[:, :listed].astype(jnp.int32).reshape(count * seg_count, K)
    high_all = meta_all[:, listed : 2 * listed].reshape(count * seg_count, K)
    low_all = meta_all[:, 2 * listed :].reshape(count * seg_count, K)
    experts = jnp.arange(E, dtype=jnp.int32)
    slots_all = jnp.sum(
        jnp.where(ids_all[:, :, None] == experts, owner_slot[None, None, :], 0), axis=2
    )
    hits = slots_all[:, :, None] == jnp.arange(count, dtype=jnp.int32)
    coef = jnp.concatenate(
        [
            jnp.sum(jnp.where(hits, high_all[:, :, None], 0.0), axis=1),
            jnp.sum(jnp.where(hits, low_all[:, :, None], 0.0), axis=1),
        ],
        axis=0,
    ).astype(jnp.bfloat16)
    halves = jnp.einsum("ms,srl->mrl", coef, by_slot, preferred_element_type=jnp.float32)
    merged_chunks = (halves[: count * seg_count] + halves[count * seg_count :]).astype(jnp.bfloat16)
    merged = join_panels(exchange(merged_chunks.reshape(count, seg_count, rows, lanes)))

    hidden_seg = hidden_act.reshape(seg_count, seg_len, ff_local)
    cot_seg = full_cot.reshape(seg_count, seg_len, width)
    seg_grads = jnp.einsum(
        "stf,std->sfd", hidden_seg, cot_seg, preferred_element_type=jnp.float32
    ).astype(jnp.bfloat16)
    returned = exchange(split_panels(seg_grads, count)).reshape(count * seg_count, rows, lanes)

    partial_rows = jnp.einsum(
        "stf,sfd->std", hidden_seg, merged, preferred_element_type=jnp.float32
    ).reshape(row_count, width)
    layer_out = lax.psum_scatter(
        partial_rows.astype(jnp.bfloat16), "tensor", scatter_dimension=1, tiled=True
    )
    grad_hidden = (
        jnp.einsum("std,sfd->stf", cot_seg, merged, preferred_element_type=jnp.float32)
        .astype(jnp.bfloat16)
        .reshape(row_count, ff_local)
    )

    by_segment = jnp.stack([coef[: count * seg_count], coef[count * seg_count :]], axis=1)
    slot_halves = jnp.einsum(
        "mhs,mrl->hsrl", by_segment, returned, preferred_element_type=jnp.float32
    )
    slot_grads = (slot_halves[0] + slot_halves[1]).astype(jnp.bfloat16)
    own_grad = join_panels(exchange(slot_grads)[:, None])
    expert_grad = jnp.transpose(own_grad, (1, 0, 2)).astype(jnp.float32)
    return (layer_out, grad_hidden, expert_grad)


def solution(mesh):
    placed = (
        P("dp", "tensor"),
        P("dp", "tensor"),
        P("tensor", "dp", None),
        P("dp", None),
        P("dp", None),
        P(),
    )
    return jax.shard_map(
        body,
        mesh=mesh,
        in_specs=placed,
        out_specs=(P("dp", "tensor"), P("dp", "tensor"), P("tensor", "dp", None)),
        check_vma=False,
    )
```

```python
import functools
import jax
import jax.numpy as jnp
from jax import lax
from jax.experimental import pallas as pl
from jax.experimental.pallas import tpu as pltpu
from jax.sharding import PartitionSpec as P

K = 4
ROW_PARTS = 4
TILE_ROWS = 16


def two_pieces(values):
    high = lax.reduce_precision(values, 8, 7)
    low = lax.reduce_precision(values - high, 8, 7)
    return high, low


def split_panels(panels, count):
    lead, ff_local, width = panels.shape
    cols = count // ROW_PARTS
    rows = ff_local // ROW_PARTS
    view = panels.reshape(lead, ROW_PARTS, rows, cols, width // cols)
    return jnp.transpose(view, (1, 3, 0, 2, 4)).reshape(count, lead * rows, width // cols)


def join_panels(chunks, lead, rows):
    count, _, lanes = chunks.shape
    cols = count // ROW_PARTS
    view = chunks[:, : lead * rows].reshape(ROW_PARTS, cols, lead, rows, lanes)
    return jnp.transpose(view, (2, 0, 3, 1, 4)).reshape(lead, ROW_PARTS * rows, cols * lanes)


def coefficients(inner, meta_row, listed, seg_count, place_ref):
    count, padded, lanes = inner.shape
    base = (meta_row // TILE_ROWS) * TILE_ROWS
    tail = inner[:, pl.ds(base, TILE_ROWS), :].astype(jnp.float32)
    which = lax.broadcasted_iota(jnp.int32, tail.shape, 1)
    meta = jnp.sum(jnp.where(which == meta_row - base, tail, 0.0), axis=1)
    lane = lax.broadcasted_iota(jnp.int32, (count, lanes), 1).astype(jnp.float32)
    found = []
    for seg in range(seg_count):
        pieces = []
        for piece in (1, 2):
            total = jnp.zeros((count, lanes), jnp.float32)
            for k in range(K):
                at = seg * K + k
                weight = meta[:, piece * listed + at : piece * listed + at + 1]
                total = total + jnp.where(lane == meta[:, at : at + 1], weight, 0.0)
            pieces.append(total)
        rows = jnp.concatenate(pieces, axis=1).astype(jnp.bfloat16)
        found.append(jnp.dot(rows, place_ref[...], preferred_element_type=jnp.float32))
    return jnp.concatenate(found, axis=0).astype(jnp.bfloat16)


def swap_body(sizes, decode, x_ref, aux_ref, wide_ref, *refs):
    rows, lead_in, lead_out = sizes
    gathers = decode is not None
    if gathers:
        out_ref, full_ref, coef_ref, inner, inner_wide, outer_wide, outer = refs[:7]
    else:
        out_ref, sum_ref, inner, inner_wide, outer_wide, outer, held = refs[:7]
    send_one, recv_one, send_two, recv_two, send_side, recv_side = refs[-6:]
    me, side = lax.axis_index("dp"), lax.axis_index("tensor")
    count, padded_in, lanes = x_ref.shape
    padded_out = out_ref.shape[1]
    sides = lax.axis_size("tensor")
    barrier = pltpu.get_barrier_semaphore()

    def greet(step, carry):
        pl.semaphore_signal(
            barrier,
            inc=1,
            device_id={"dp": lax.rem(me + step, count)},
            device_id_type=pl.DeviceIdType.MESH,
        )
        return carry

    def greet_side(step, carry):
        pl.semaphore_signal(
            barrier,
            inc=1,
            device_id={"tensor": lax.rem(side + step, sides)},
            device_id_type=pl.DeviceIdType.MESH,
        )
        return carry

    lax.fori_loop(1, count, greet, 0)
    lax.fori_loop(1, sides, greet_side, 0)
    pl.semaphore_wait(barrier, count + sides - 2)

    def copies(source, target, send_sem, recv_sem):
        def copy(step):
            peer = lax.rem(me + step, count)
            return pltpu.make_async_remote_copy(
                src_ref=source.at[peer],
                dst_ref=target.at[me],
                send_sem=send_sem.at[step],
                recv_sem=recv_sem.at[step],
                device_id={"dp": peer},
                device_id_type=pl.DeviceIdType.MESH,
            )

        return copy

    def stripe(index):
        part = wide_ref.shape[1] if gathers else sum_ref.shape[1]
        return pl.ds(pl.multiple_of(index * part, 128), part)

    def side_copy(step):
        peer = lax.rem(side + step, sides)
        return pltpu.make_async_remote_copy(
            src_ref=wide_ref if gathers else wide_ref.at[:, stripe(peer)],
            dst_ref=full_ref.at[:, stripe(side)] if gathers else held.at[side],
            send_sem=send_side.at[step],
            recv_sem=recv_side.at[step],
            device_id={"tensor": peer},
            device_id_type=pl.DeviceIdType.MESH,
        )

    def begin(copy, steps):
        def one(step, carry):
            copy(step).start()
            return carry

        lax.fori_loop(1, steps, one, 0)

    def finish(copy, steps):
        def one(step, carry):
            copy(step).wait()
            return carry

        lax.fori_loop(1, steps, one, 0)

    first = copies(x_ref, inner, send_one, recv_one)
    begin(first, count)
    begin(side_copy, sides)
    inner[pl.ds(me, 1)] = x_ref[pl.ds(me, 1)]
    if gathers:
        full_ref[:, stripe(side)] = wide_ref[...]
    else:
        held[pl.ds(side, 1)] = wide_ref[:, stripe(side)][None]
    finish(first, count)
    if gathers:
        coef = coefficients(inner, *decode, aux_ref)
        coef_ref[...] = coef
    else:
        coef = aux_ref[...]
    inner_wide[...] = inner[...].astype(jnp.float32).reshape(count * padded_in, lanes)
    outer_wide[...] = jnp.zeros_like(outer_wide)
    for row in range(0, rows, 2):
        pair = jnp.concatenate(
            [
                jnp.concatenate(
                    [
                        inner_wide[pl.ds(seg * rows + row + i, count, stride=padded_in), :]
                        for seg in range(lead_in)
                    ],
                    axis=0,
                )
                for i in (0, 1)
            ],
            axis=1,
        ).astype(jnp.bfloat16)
        summed = jnp.dot(
            coef, jnp.concatenate([pair, pair], axis=0), preferred_element_type=jnp.float32
        )
        for seg in range(lead_out):
            for i in (0, 1):
                outer_wide[pl.ds(seg * rows + row + i, count, stride=padded_out), :] = summed[
                    seg * count : (seg + 1) * count, i * lanes : (i + 1) * lanes
                ]
    outer[...] = outer_wide[...].reshape(count, padded_out, lanes).astype(jnp.bfloat16)
    second = copies(outer, out_ref, send_two, recv_two)
    begin(second, count)
    out_ref[pl.ds(me, 1)] = outer[pl.ds(me, 1)]
    finish(side_copy, sides)
    if not gathers:
        height = 64

        def add_up(block, carry):
            at = pl.ds(pl.multiple_of(block * height, height), height)
            total = held[0, at, :].astype(jnp.float32)
            for other in range(1, sides):
                total = total + held[other, at, :].astype(jnp.float32)
            sum_ref[at, :] = total.astype(sum_ref.dtype)
            return carry

        lax.fori_loop(0, sum_ref.shape[0] // height, add_up, 0)
    finish(second, count)


def swap(blocks, aux, wide, rows, lead_in, lead_out, decode, collective_id):
    count, padded_in, lanes = blocks.shape
    padded_out = -(-lead_out * rows // 8) * 8
    sides = lax.axis_size("tensor")
    tall, across = wide.shape
    if decode is not None:
        side_shapes = (
            jax.ShapeDtypeStruct((tall, across * sides), jnp.bfloat16),
            jax.ShapeDtypeStruct((lead_out * count, 2 * count), jnp.bfloat16),
        )
        holds = []
    else:
        side_shapes = (jax.ShapeDtypeStruct((tall, across // sides), jnp.bfloat16),)
        holds = [pltpu.VMEM((sides, tall, across // sides), jnp.bfloat16)]
    results = (jax.ShapeDtypeStruct((count, padded_out, lanes), jnp.bfloat16),) + side_shapes
    vmem = pl.BlockSpec(memory_space=pltpu.VMEM)
    return pl.pallas_call(
        functools.partial(swap_body, (rows, lead_in, lead_out), decode),
        out_shape=results,
        in_specs=[vmem] * 3,
        out_specs=(vmem,) * len(results),
        scratch_shapes=[
            pltpu.VMEM((count, padded_in, lanes), jnp.bfloat16),
            pltpu.VMEM((count * padded_in, lanes), jnp.float32),
            pltpu.VMEM((count * padded_out, lanes), jnp.float32),
            pltpu.VMEM((count, padded_out, lanes), jnp.bfloat16),
        ]
        + holds
        + [pltpu.SemaphoreType.DMA((count,))] * 4
        + [pltpu.SemaphoreType.DMA((sides,))] * 2,
        compiler_params=pltpu.CompilerParams(
            collective_id=collective_id, has_side_effects=True, vmem_limit_bytes=40 * 1024 * 1024
        ),
    )(blocks, aux, wide)


def body(hidden_act, cotangent, down_table, expert_ids, merge_weights, owner_slot):
    count = lax.axis_size("dp")
    seg_count = expert_ids.shape[0]
    ff_local, _, width = down_table.shape
    row_count = hidden_act.shape[0]
    seg_len = row_count // seg_count
    rows = ff_local // ROW_PARTS
    padded = -(-(rows + 1) // 8) * 8
    lanes = width * ROW_PARTS // count
    listed = seg_count * K

    high, low = two_pieces(merge_weights)
    meta = jnp.concatenate(
        [expert_ids.astype(jnp.float32).reshape(-1), high.reshape(-1), low.reshape(-1)]
    ).astype(jnp.bfloat16)
    meta = jnp.pad(meta[None, :], ((0, padded - rows - 1), (0, lanes - 3 * listed)))
    table_chunks = split_panels(jnp.transpose(down_table, (1, 0, 2)), count)
    outgoing = jnp.concatenate(
        [table_chunks, jnp.broadcast_to(meta, (count,) + meta.shape)], axis=1
    )
    slot_range = jnp.arange(count, dtype=jnp.int32)
    place = jnp.pad(
        (owner_slot[:, None] == slot_range[None, :]).astype(jnp.bfloat16),
        ((0, lanes - owner_slot.shape[0]), (0, 0)),
    )
    nothing = jnp.zeros_like(place)
    place_two = jnp.concatenate(
        [
            jnp.concatenate([place, nothing], axis=1),
            jnp.concatenate([nothing, place], axis=1),
        ],
        axis=0,
    )
    merged_chunks, full_cot, coef = swap(
        outgoing, place_two, cotangent, rows, 1, seg_count, (rows, listed, seg_count), 0
    )
    merged = join_panels(merged_chunks, seg_count, rows)

    hidden_seg = hidden_act.reshape(seg_count, seg_len, ff_local)
    cot_seg = full_cot.reshape(seg_count, seg_len, width)
    seg_grads = jnp.einsum(
        "stf,std->sfd", hidden_seg, cot_seg, preferred_element_type=jnp.float32
    ).astype(jnp.bfloat16)

    partial_rows = jnp.einsum(
        "stf,sfd->std", hidden_seg, merged, preferred_element_type=jnp.float32
    ).reshape(row_count, width)
    grad_hidden = (
        jnp.einsum("std,sfd->stf", cot_seg, merged, preferred_element_type=jnp.float32)
        .astype(jnp.bfloat16)
        .reshape(row_count, ff_local)
    )

    by_segment = jnp.transpose(
        coef.reshape(seg_count * count, 2, count), (2, 1, 0)
    ).reshape(count, 2 * seg_count * count)
    slot_chunks, layer_out = swap(
        split_panels(seg_grads, count),
        by_segment,
        partial_rows.astype(jnp.bfloat16),
        rows,
        seg_count,
        1,
        None,
        1,
    )
    own_grad = join_panels(slot_chunks, 1, rows)
    expert_grad = jnp.transpose(own_grad, (1, 0, 2)).astype(jnp.float32)
    return (layer_out, grad_hidden, expert_grad)


def solution(mesh):
    placed = (
        P("dp", "tensor"),
        P("dp", "tensor"),
        P("tensor", "dp", None),
        P("dp", None),
        P("dp", None),
        P(),
    )
    return jax.shard_map(
        body,
        mesh=mesh,
        in_specs=placed,
        out_specs=(P("dp", "tensor"), P("dp", "tensor"), P("tensor", "dp", None)),
        check_vma=False,
    )
```

```python
import functools
import jax
import jax.numpy as jnp
from jax import lax
from jax.experimental import pallas as pl
from jax.experimental.pallas import tpu as pltpu
from jax.sharding import PartitionSpec as P

K = 4
ROW_PARTS = 4
TILE_ROWS = 16


def two_pieces(values):
    high = lax.reduce_precision(values, 8, 7)
    low = lax.reduce_precision(values - high, 8, 7)
    return high, low


def split_panels(panels, count):
    lead, ff_local, width = panels.shape
    cols = count // ROW_PARTS
    rows = ff_local // ROW_PARTS
    view = panels.reshape(lead, ROW_PARTS, rows, cols, width // cols)
    return jnp.transpose(view, (1, 3, 0, 2, 4)).reshape(count, lead * rows, width // cols)


def join_panels(chunks, lead, rows):
    count, _, lanes = chunks.shape
    cols = count // ROW_PARTS
    view = chunks[:, : lead * rows].reshape(ROW_PARTS, cols, lead, rows, lanes)
    return jnp.transpose(view, (2, 0, 3, 1, 4)).reshape(lead, ROW_PARTS * rows, cols * lanes)


def coefficients(inner, meta_row, listed, seg_count, place_ref):
    count, padded, lanes = inner.shape
    base = (meta_row // TILE_ROWS) * TILE_ROWS
    tail = inner[:, pl.ds(base, TILE_ROWS), :].astype(jnp.float32)
    which = lax.broadcasted_iota(jnp.int32, tail.shape, 1)
    meta = jnp.sum(jnp.where(which == meta_row - base, tail, 0.0), axis=1)
    lane = lax.broadcasted_iota(jnp.int32, (count, lanes), 1).astype(jnp.float32)
    found = []
    for seg in range(seg_count):
        pieces = []
        for piece in (1, 2):
            total = jnp.zeros((count, lanes), jnp.float32)
            for k in range(K):
                at = seg * K + k
                weight = meta[:, piece * listed + at : piece * listed + at + 1]
                total = total + jnp.where(lane == meta[:, at : at + 1], weight, 0.0)
            pieces.append(total)
        rows = jnp.concatenate(pieces, axis=1).astype(jnp.bfloat16)
        found.append(jnp.dot(rows, place_ref[...], preferred_element_type=jnp.float32))
    return jnp.concatenate(found, axis=0)


def step_body(
    rows, seg_count, decode, x_ref, place_ref, cot_ref, hid_ref, hid_t_ref,
    slot_ref, layer_ref, grad_ref,
    full, in_one, in_two, in_three, held, wide_one, wide_two, out_two, out_three, out_four,
    merged, partial, *sems
):
    me, side = lax.axis_index("dp"), lax.axis_index("tensor")
    count, padded, lanes = x_ref.shape
    tall, part = cot_ref.shape
    width = full.shape[1]
    sides = lax.axis_size("tensor")
    both = seg_count * rows
    cols = count // ROW_PARTS
    pair_lanes = 2 * lanes
    barrier = pltpu.get_barrier_semaphore()

    def greet(step, carry):
        pl.semaphore_signal(
            barrier,
            inc=1,
            device_id={"dp": lax.rem(me + step, count)},
            device_id_type=pl.DeviceIdType.MESH,
        )
        return carry

    def greet_side(step, carry):
        pl.semaphore_signal(
            barrier,
            inc=1,
            device_id={"tensor": lax.rem(side + step, sides)},
            device_id_type=pl.DeviceIdType.MESH,
        )
        return carry

    lax.fori_loop(1, count, greet, 0)
    lax.fori_loop(1, sides, greet_side, 0)
    pl.semaphore_wait(barrier, count + sides - 2)

    def copies(source, target, send_sem, recv_sem):
        def copy(step):
            peer = lax.rem(me + step, count)
            return pltpu.make_async_remote_copy(
                src_ref=source.at[peer],
                dst_ref=target.at[me],
                send_sem=send_sem.at[step],
                recv_sem=recv_sem.at[step],
                device_id={"dp": peer},
                device_id_type=pl.DeviceIdType.MESH,
            )

        return copy

    def stripe(index):
        return pl.ds(pl.multiple_of(index * part, 128), part)

    def gather_copy(step):
        return pltpu.make_async_remote_copy(
            src_ref=cot_ref,
            dst_ref=full.at[:, stripe(side)],
            send_sem=sems[8].at[step],
            recv_sem=sems[9].at[step],
            device_id={"tensor": lax.rem(side + step, sides)},
            device_id_type=pl.DeviceIdType.MESH,
        )

    def scatter_copy(step):
        peer = lax.rem(side + step, sides)
        return pltpu.make_async_remote_copy(
            src_ref=partial.at[:, stripe(peer)],
            dst_ref=held.at[side],
            send_sem=sems[10].at[step],
            recv_sem=sems[11].at[step],
            device_id={"tensor": peer},
            device_id_type=pl.DeviceIdType.MESH,
        )

    def begin(copy, steps):
        def one(step, carry):
            copy(step).start()
            return carry

        lax.fori_loop(1, steps, one, 0)

    def finish(copy, steps):
        def one(step, carry):
            copy(step).wait()
            return carry

        lax.fori_loop(1, steps, one, 0)

    def mix(coef, source, target, lead_in, lead_out, high_in, high_out):
        for row in range(0, rows, 2):
            pair = jnp.concatenate(
                [
                    jnp.concatenate(
                        [
                            source[pl.ds(seg * rows + row + i, count, stride=high_in), :]
                            for seg in range(lead_in)
                        ],
                        axis=0,
                    )
                    for i in (0, 1)
                ],
                axis=1,
            ).astype(jnp.bfloat16)
            summed = jnp.dot(
                coef, jnp.concatenate([pair, pair], axis=0), preferred_element_type=jnp.float32
            )
            for seg in range(lead_out):
                for i in (0, 1):
                    target[pl.ds(seg * rows + row + i, count, stride=high_out), :] = summed[
                        seg * count : (seg + 1) * count, i * lanes : (i + 1) * lanes
                    ]

    first = copies(x_ref, in_one, sems[0], sems[1])
    second = copies(out_two, in_two, sems[2], sems[3])
    third = copies(out_three, in_three, sems[4], sems[5])
    fourth = copies(out_four, slot_ref, sems[6], sems[7])

    begin(first, count)
    begin(gather_copy, sides)
    in_one[pl.ds(me, 1)] = x_ref[pl.ds(me, 1)]
    full[:, stripe(side)] = cot_ref[...]
    finish(first, count)

    coef = coefficients(in_one, *decode, place_ref)
    wide_one[...] = in_one[...].astype(jnp.float32).reshape(count * padded, lanes)
    mix(coef.astype(jnp.bfloat16), wide_one, wide_two, 1, seg_count, padded, both)
    out_two[...] = wide_two[...].reshape(count, both, lanes).astype(jnp.bfloat16)
    begin(second, count)
    in_two[pl.ds(me, 1)] = out_two[pl.ds(me, 1)]

    finish(gather_copy, sides)

    def seg_grads(block, carry):
        at = pl.ds(pl.multiple_of(block * pair_lanes, pair_lanes), pair_lanes)
        product = jnp.dot(hid_t_ref[...], full[:, at], preferred_element_type=jnp.float32)
        for up in range(ROW_PARTS):
            for i in (0, 1):
                out_three[pl.ds(up * cols + block * 2 + i, 1)] = product[
                    up * both : (up + 1) * both, i * lanes : (i + 1) * lanes
                ].astype(jnp.bfloat16)[None]
        return carry

    lax.fori_loop(0, width // pair_lanes, seg_grads, 0)
    begin(third, count)
    in_three[pl.ds(me, 1)] = out_three[pl.ds(me, 1)]

    finish(second, count)
    wide_two[...] = in_two[...].astype(jnp.float32).reshape(count * both, lanes)

    def forward(block, carry):
        at = pl.ds(pl.multiple_of(block * pair_lanes, pair_lanes), pair_lanes)
        panel = jnp.concatenate(
            [
                jnp.concatenate(
                    [
                        wide_two[
                            pl.ds(
                                pl.multiple_of((up * cols + block * 2 + i) * both, 8), both
                            ),
                            :,
                        ]
                        for up in range(ROW_PARTS)
                    ],
                    axis=0,
                )
                for i in (0, 1)
            ],
            axis=1,
        ).astype(jnp.bfloat16)
        merged[:, at] = panel
        partial[:, at] = jnp.dot(
            hid_ref[...], panel, preferred_element_type=jnp.float32
        ).astype(jnp.bfloat16)
        return carry

    lax.fori_loop(0, width // pair_lanes, forward, 0)
    begin(scatter_copy, sides)
    held[pl.ds(side, 1)] = partial[:, stripe(side)][None]

    height = 64

    def backward(block, carry):
        at = pl.ds(pl.multiple_of(block * height, height), height)
        grad_ref[at, :] = lax.dot_general(
            full[at, :],
            merged[...],
            (((1,), (1,)), ((), ())),
            preferred_element_type=jnp.float32,
        ).astype(jnp.bfloat16)
        return carry

    lax.fori_loop(0, tall // height, backward, 0)

    finish(third, count)
    turned = jnp.transpose(coef)
    by_segment = jnp.concatenate([turned[:count], turned[count:]], axis=1)
    wide_two[...] = in_three[...].astype(jnp.float32).reshape(count * both, lanes)
    wide_one[...] = jnp.zeros_like(wide_one)
    mix(by_segment.astype(jnp.bfloat16), wide_two, wide_one, seg_count, 1, both, padded)
    out_four[...] = wide_one[...].reshape(count, padded, lanes).astype(jnp.bfloat16)
    begin(fourth, count)
    slot_ref[pl.ds(me, 1)] = out_four[pl.ds(me, 1)]

    finish(scatter_copy, sides)

    def add_up(block, carry):
        at = pl.ds(pl.multiple_of(block * height, height), height)
        total = held[0, at, :].astype(jnp.float32)
        for other in range(1, sides):
            total = total + held[other, at, :].astype(jnp.float32)
        layer_ref[at, :] = total.astype(jnp.bfloat16)
        return carry

    lax.fori_loop(0, tall // height, add_up, 0)
    finish(fourth, count)


def whole_step(blocks, place, cotangent, hidden, hidden_t, rows, seg_count, decode):
    count, padded, lanes = blocks.shape
    sides = lax.axis_size("tensor")
    tall, part = cotangent.shape
    both = seg_count * rows
    high = ROW_PARTS * both
    vmem = pl.BlockSpec(memory_space=pltpu.VMEM)
    narrow = functools.partial(pltpu.VMEM, dtype=jnp.bfloat16)
    results = tuple(
        jax.ShapeDtypeStruct(shape, jnp.bfloat16)
        for shape in ((count, padded, lanes), (tall, part), (tall, high))
    )
    return pl.pallas_call(
        functools.partial(step_body, rows, seg_count, decode),
        out_shape=results,
        in_specs=[vmem] * 5,
        out_specs=(vmem,) * 3,
        scratch_shapes=[
            narrow((tall, part * sides)),
            narrow((count, padded, lanes)),
            narrow((count, both, lanes)),
            narrow((count, both, lanes)),
            narrow((sides, tall, part)),
            pltpu.VMEM((count * padded, lanes), jnp.float32),
            pltpu.VMEM((count * both, lanes), jnp.float32),
            narrow((count, both, lanes)),
            narrow((count, both, lanes)),
            narrow((count, padded, lanes)),
            narrow((high, part * sides)),
            narrow((tall, part * sides)),
        ]
        + [pltpu.SemaphoreType.DMA((count,))] * 8
        + [pltpu.SemaphoreType.DMA((sides,))] * 4,
        compiler_params=pltpu.CompilerParams(
            collective_id=0, has_side_effects=True, vmem_limit_bytes=56 * 1024 * 1024
        ),
    )(blocks, place, cotangent, hidden, hidden_t)


def body(hidden_act, cotangent, down_table, expert_ids, merge_weights, owner_slot):
    count = lax.axis_size("dp")
    seg_count = expert_ids.shape[0]
    ff_local, _, width = down_table.shape
    row_count = hidden_act.shape[0]
    seg_len = row_count // seg_count
    rows = ff_local // ROW_PARTS
    padded = -(-(rows + 1) // 8) * 8
    lanes = width * ROW_PARTS // count
    listed = seg_count * K

    high, low = two_pieces(merge_weights)
    meta = jnp.concatenate(
        [expert_ids.astype(jnp.float32).reshape(-1), high.reshape(-1), low.reshape(-1)]
    ).astype(jnp.bfloat16)
    meta = jnp.pad(meta[None, :], ((0, padded - rows - 1), (0, lanes - 3 * listed)))
    table_chunks = split_panels(jnp.transpose(down_table, (1, 0, 2)), count)
    outgoing = jnp.concatenate(
        [table_chunks, jnp.broadcast_to(meta, (count,) + meta.shape)], axis=1
    )
    slot_range = jnp.arange(count, dtype=jnp.int32)
    place = jnp.pad(
        (owner_slot[:, None] == slot_range[None, :]).astype(jnp.bfloat16),
        ((0, lanes - owner_slot.shape[0]), (0, 0)),
    )
    nothing = jnp.zeros_like(place)
    place_two = jnp.concatenate(
        [
            jnp.concatenate([place, nothing], axis=1),
            jnp.concatenate([nothing, place], axis=1),
        ],
        axis=0,
    )
    parts = hidden_act.reshape(seg_count, seg_len, ROW_PARTS, 1, rows)
    same = jnp.eye(seg_count, dtype=jnp.bool_)[:, None, None, :, None]
    hidden = jnp.where(same, parts, 0).reshape(row_count, ROW_PARTS * seg_count * rows)
    slot_chunks, layer_out, grad_all = whole_step(
        outgoing,
        place_two,
        cotangent,
        hidden,
        hidden.T,
        rows,
        seg_count,
        (rows, listed, seg_count),
    )
    grad_view = grad_all.reshape(seg_count, seg_len, ROW_PARTS, seg_count, rows)
    grad_hidden = jnp.stack(
        [grad_view[seg, :, :, seg] for seg in range(seg_count)]
    ).reshape(row_count, ff_local)
    own_grad = join_panels(slot_chunks, 1, rows)
    expert_grad = jnp.transpose(own_grad, (1, 0, 2)).astype(jnp.float32)
    return (layer_out, grad_hidden, expert_grad)


def solution(mesh):
    placed = (
        P("dp", "tensor"),
        P("dp", "tensor"),
        P("tensor", "dp", None),
        P("dp", None),
        P("dp", None),
        P(),
    )
    return jax.shard_map(
        body,
        mesh=mesh,
        in_specs=placed,
        out_specs=(P("dp", "tensor"), P("dp", "tensor"), P("tensor", "dp", None)),
        check_vma=False,
    )
```

```python
import functools
import jax
import jax.numpy as jnp
from jax import lax
from jax.experimental import pallas as pl
from jax.experimental.pallas import tpu as pltpu
from jax.sharding import PartitionSpec as P

K = 4
ROW_PARTS = 4
TILE_ROWS = 16


def two_pieces(values):
    high = lax.reduce_precision(values, 8, 7)
    low = lax.reduce_precision(values - high, 8, 7)
    return high, low


def split_panels(panels, count):
    lead, ff_local, width = panels.shape
    cols = count // ROW_PARTS
    rows = ff_local // ROW_PARTS
    view = panels.reshape(lead, ROW_PARTS, rows, cols, width // cols)
    return jnp.transpose(view, (1, 3, 0, 2, 4)).reshape(count, lead * rows, width // cols)


def join_panels(chunks, lead, rows):
    count, high, lanes = chunks.shape
    cols = count // ROW_PARTS
    view = chunks[:, high - lead * rows :].reshape(ROW_PARTS, cols, lead, rows, lanes)
    return jnp.transpose(view, (2, 0, 3, 1, 4)).reshape(lead, ROW_PARTS * rows, cols * lanes)


def coefficients(inner, meta_row, listed, seg_count, place_ref):
    count, padded, lanes = inner.shape
    base = (meta_row // TILE_ROWS) * TILE_ROWS
    tail = inner[:, pl.ds(base, TILE_ROWS), :].astype(jnp.float32)
    which = lax.broadcasted_iota(jnp.int32, tail.shape, 1)
    meta = jnp.sum(jnp.where(which == meta_row - base, tail, 0.0), axis=1)
    lane = lax.broadcasted_iota(jnp.int32, (count, lanes), 1).astype(jnp.float32)
    found = []
    for seg in range(seg_count):
        pieces = []
        for piece in (1, 2):
            total = jnp.zeros((count, lanes), jnp.float32)
            for k in range(K):
                at = seg * K + k
                weight = meta[:, piece * listed + at : piece * listed + at + 1]
                total = total + jnp.where(lane == meta[:, at : at + 1], weight, 0.0)
            pieces.append(total)
        rows = jnp.concatenate(pieces, axis=1).astype(jnp.bfloat16)
        found.append(jnp.dot(rows, place_ref[...], preferred_element_type=jnp.float32))
    return jnp.concatenate(found, axis=0)


def step_body(
    rows, seg_count, decode, x_ref, place_ref, cot_ref, hid_ref, hid_t_ref,
    slot_ref, layer_ref, grad_ref,
    full, in_one, in_two, in_three, held, wide_one, wide_two, out_two, out_three, out_four,
    merged, partial, *sems
):
    me, side = lax.axis_index("dp"), lax.axis_index("tensor")
    count, padded, lanes = x_ref.shape
    tall, part = cot_ref.shape
    width = full.shape[1]
    sides = lax.axis_size("tensor")
    both = seg_count * rows
    cols = count // ROW_PARTS
    pair_lanes = 2 * lanes
    barrier = pltpu.get_barrier_semaphore()

    def greet(step, carry):
        pl.semaphore_signal(
            barrier,
            inc=1,
            device_id={"dp": lax.rem(me + step, count)},
            device_id_type=pl.DeviceIdType.MESH,
        )
        return carry

    def greet_side(step, carry):
        pl.semaphore_signal(
            barrier,
            inc=1,
            device_id={"tensor": lax.rem(side + step, sides)},
            device_id_type=pl.DeviceIdType.MESH,
        )
        return carry

    lax.fori_loop(1, count, greet, 0)
    lax.fori_loop(1, sides, greet_side, 0)
    pl.semaphore_wait(barrier, count + sides - 2)

    half = padded // 2
    cut = half - (padded - rows)
    slim = ((0, half), (half, half))
    double = ((0, seg_count * cut), (seg_count * cut, seg_count * (rows - cut)))

    def copies(source, target, send_sem, recv_sem, piece, piece_index):
        def copy(step):
            peer = lax.rem(me + step, count)
            mark = piece_index * count + step
            return pltpu.make_async_remote_copy(
                src_ref=source.at[peer, pl.ds(*piece)],
                dst_ref=target.at[me, pl.ds(*piece)],
                send_sem=send_sem.at[mark],
                recv_sem=recv_sem.at[mark],
                device_id={"dp": peer},
                device_id_type=pl.DeviceIdType.MESH,
            )

        return copy

    def stripe(index):
        return pl.ds(pl.multiple_of(index * part, 128), part)

    def gather_copy(step):
        return pltpu.make_async_remote_copy(
            src_ref=cot_ref,
            dst_ref=full.at[:, stripe(side)],
            send_sem=sems[8].at[step],
            recv_sem=sems[9].at[step],
            device_id={"tensor": lax.rem(side + step, sides)},
            device_id_type=pl.DeviceIdType.MESH,
        )

    def scatter_copy(step):
        peer = lax.rem(side + step, sides)
        return pltpu.make_async_remote_copy(
            src_ref=partial.at[:, stripe(peer)],
            dst_ref=held.at[side],
            send_sem=sems[10].at[step],
            recv_sem=sems[11].at[step],
            device_id={"tensor": peer},
            device_id_type=pl.DeviceIdType.MESH,
        )

    def begin(copy, steps):
        def one(step, carry):
            copy(step).start()
            return carry

        lax.fori_loop(1, steps, one, 0)

    def finish(copy, steps):
        def one(step, carry):
            copy(step).wait()
            return carry

        lax.fori_loop(1, steps, one, 0)

    def spot(piece, seg, row, lead):
        if lead == 1:
            return row + padded - rows - piece * half
        return seg * (rows - cut) + row - cut if piece else seg * cut + row

    def mix(coef, piece, source, target, lead_in, lead_out):
        start_in, high_in = (double if lead_in > 1 else slim)[piece]
        start_out, high_out = (double if lead_out > 1 else slim)[piece]
        for row in range(cut if piece else 0, rows if piece else cut, 2):
            pair = jnp.concatenate(
                [
                    jnp.concatenate(
                        [
                            source[
                                pl.ds(
                                    count * start_in + spot(piece, seg, row + i, lead_in),
                                    count,
                                    stride=high_in,
                                ),
                                :,
                            ]
                            for seg in range(lead_in)
                        ],
                        axis=0,
                    )
                    for i in (0, 1)
                ],
                axis=1,
            ).astype(jnp.bfloat16)
            summed = jnp.dot(
                coef, jnp.concatenate([pair, pair], axis=0), preferred_element_type=jnp.float32
            )
            for seg in range(lead_out):
                for i in (0, 1):
                    target[
                        pl.ds(
                            count * start_out + spot(piece, seg, row + i, lead_out),
                            count,
                            stride=high_out,
                        ),
                        :,
                    ] = summed[seg * count : (seg + 1) * count, i * lanes : (i + 1) * lanes]

    def widen(source, target, piece):
        start, high = piece
        target[pl.ds(count * start, count * high), :] = (
            source[:, pl.ds(start, high), :].astype(jnp.float32).reshape(count * high, lanes)
        )

    def narrow(source, target, piece):
        start, high = piece
        target[:, pl.ds(start, high), :] = (
            source[pl.ds(count * start, count * high), :]
            .reshape(count, high, lanes)
            .astype(jnp.bfloat16)
        )

    first = [copies(x_ref, in_one, sems[0], sems[1], slim[p], p) for p in (0, 1)]
    second = [copies(out_two, in_two, sems[2], sems[3], double[p], p) for p in (0, 1)]
    third = [copies(out_three, in_three, sems[4], sems[5], double[p], p) for p in (0, 1)]
    fourth = [copies(out_four, slot_ref, sems[6], sems[7], slim[p], p) for p in (0, 1)]

    begin(first[0], count)
    begin(first[1], count)
    begin(gather_copy, sides)
    in_one[pl.ds(me, 1)] = x_ref[pl.ds(me, 1)]
    full[:, stripe(side)] = cot_ref[...]
    finish(first[0], count)
    coef = coefficients(in_one, *decode, place_ref)
    for p in (0, 1):
        if p:
            finish(first[1], count)
        widen(in_one, wide_one, slim[p])
        mix(coef.astype(jnp.bfloat16), p, wide_one, wide_two, 1, seg_count)
        narrow(wide_two, out_two, double[p])
        begin(second[p], count)
    in_two[pl.ds(me, 1)] = out_two[pl.ds(me, 1)]

    finish(gather_copy, sides)

    def seg_grads(block, carry):
        at = pl.ds(pl.multiple_of(block * pair_lanes, pair_lanes), pair_lanes)
        product = jnp.dot(hid_t_ref[...], full[:, at], preferred_element_type=jnp.float32)
        for up in range(ROW_PARTS):
            for i in (0, 1):
                out_three[pl.ds(up * cols + block * 2 + i, 1)] = product[
                    up * both : (up + 1) * both, i * lanes : (i + 1) * lanes
                ].astype(jnp.bfloat16)[None]
        return carry

    lax.fori_loop(0, width // pair_lanes, seg_grads, 0)
    begin(third[0], count)
    begin(third[1], count)
    in_three[pl.ds(me, 1)] = out_three[pl.ds(me, 1)]

    finish(second[0], count)
    finish(second[1], count)
    wide_two[...] = in_two[...].astype(jnp.float32).reshape(count * both, lanes)

    def forward(block, carry):
        at = pl.ds(pl.multiple_of(block * pair_lanes, pair_lanes), pair_lanes)
        panel = jnp.concatenate(
            [
                jnp.concatenate(
                    [
                        wide_two[
                            pl.ds(
                                pl.multiple_of((up * cols + block * 2 + i) * both, 8), both
                            ),
                            :,
                        ]
                        for up in range(ROW_PARTS)
                    ],
                    axis=0,
                )
                for i in (0, 1)
            ],
            axis=1,
        ).astype(jnp.bfloat16)
        merged[:, at] = panel
        partial[:, at] = jnp.dot(
            hid_ref[...], panel, preferred_element_type=jnp.float32
        ).astype(jnp.bfloat16)
        return carry

    lax.fori_loop(0, width // pair_lanes, forward, 0)
    begin(scatter_copy, sides)
    held[pl.ds(side, 1)] = partial[:, stripe(side)][None]

    height = 64

    def backward(block, carry):
        at = pl.ds(pl.multiple_of(block * height, height), height)
        grad_ref[at, :] = lax.dot_general(
            full[at, :],
            merged[...],
            (((1,), (1,)), ((), ())),
            preferred_element_type=jnp.float32,
        ).astype(jnp.bfloat16)
        return carry

    lax.fori_loop(0, tall // height, backward, 0)

    turned = jnp.transpose(coef)
    by_segment = jnp.concatenate([turned[:count], turned[count:]], axis=1)
    wide_one[...] = jnp.zeros_like(wide_one)
    for p in (0, 1):
        finish(third[p], count)
        widen(in_three, wide_two, double[p])
        mix(by_segment.astype(jnp.bfloat16), p, wide_two, wide_one, seg_count, 1)
        narrow(wide_one, out_four, slim[p])
        begin(fourth[p], count)
    slot_ref[pl.ds(me, 1)] = out_four[pl.ds(me, 1)]

    finish(scatter_copy, sides)

    def add_up(block, carry):
        at = pl.ds(pl.multiple_of(block * height, height), height)
        total = held[0, at, :].astype(jnp.float32)
        for other in range(1, sides):
            total = total + held[other, at, :].astype(jnp.float32)
        layer_ref[at, :] = total.astype(jnp.bfloat16)
        return carry

    lax.fori_loop(0, tall // height, add_up, 0)
    finish(fourth[0], count)
    finish(fourth[1], count)


def whole_step(blocks, place, cotangent, hidden, hidden_t, rows, seg_count, decode):
    count, padded, lanes = blocks.shape
    sides = lax.axis_size("tensor")
    tall, part = cotangent.shape
    both = seg_count * rows
    high = ROW_PARTS * both
    vmem = pl.BlockSpec(memory_space=pltpu.VMEM)
    narrow = functools.partial(pltpu.VMEM, dtype=jnp.bfloat16)
    results = tuple(
        jax.ShapeDtypeStruct(shape, jnp.bfloat16)
        for shape in ((count, padded, lanes), (tall, part), (tall, high))
    )
    return pl.pallas_call(
        functools.partial(step_body, rows, seg_count, decode),
        out_shape=results,
        in_specs=[vmem] * 5,
        out_specs=(vmem,) * 3,
        scratch_shapes=[
            narrow((tall, part * sides)),
            narrow((count, padded, lanes)),
            narrow((count, both, lanes)),
            narrow((count, both, lanes)),
            narrow((sides, tall, part)),
            pltpu.VMEM((count * padded, lanes), jnp.float32),
            pltpu.VMEM((count * both, lanes), jnp.float32),
            narrow((count, both, lanes)),
            narrow((count, both, lanes)),
            narrow((count, padded, lanes)),
            narrow((high, part * sides)),
            narrow((tall, part * sides)),
        ]
        + [pltpu.SemaphoreType.DMA((2 * count,))] * 8
        + [pltpu.SemaphoreType.DMA((sides,))] * 4,
        compiler_params=pltpu.CompilerParams(
            collective_id=0, has_side_effects=True, vmem_limit_bytes=56 * 1024 * 1024
        ),
    )(blocks, place, cotangent, hidden, hidden_t)


def body(hidden_act, cotangent, down_table, expert_ids, merge_weights, owner_slot):
    count = lax.axis_size("dp")
    seg_count = expert_ids.shape[0]
    ff_local, _, width = down_table.shape
    row_count = hidden_act.shape[0]
    seg_len = row_count // seg_count
    rows = ff_local // ROW_PARTS
    padded = -(-(rows + 1) // 8) * 8
    lanes = width * ROW_PARTS // count
    listed = seg_count * K

    high, low = two_pieces(merge_weights)
    meta = jnp.concatenate(
        [expert_ids.astype(jnp.float32).reshape(-1), high.reshape(-1), low.reshape(-1)]
    ).astype(jnp.bfloat16)
    meta = jnp.pad(meta[None, :], ((0, padded - rows - 1), (0, lanes - 3 * listed)))
    table_chunks = split_panels(jnp.transpose(down_table, (1, 0, 2)), count)
    outgoing = jnp.concatenate(
        [jnp.broadcast_to(meta, (count,) + meta.shape), table_chunks], axis=1
    )
    slot_range = jnp.arange(count, dtype=jnp.int32)
    place = jnp.pad(
        (owner_slot[:, None] == slot_range[None, :]).astype(jnp.bfloat16),
        ((0, lanes - owner_slot.shape[0]), (0, 0)),
    )
    nothing = jnp.zeros_like(place)
    place_two = jnp.concatenate(
        [
            jnp.concatenate([place, nothing], axis=1),
            jnp.concatenate([nothing, place], axis=1),
        ],
        axis=0,
    )
    cut = padded // 2 - (padded - rows)
    parts = hidden_act.reshape(seg_count, seg_len, ROW_PARTS, 1, rows)
    same = jnp.eye(seg_count, dtype=jnp.bool_)[:, None, None, :, None]
    spread = jnp.where(same, parts, 0)
    lead_shape = (row_count, ROW_PARTS, -1)
    hidden = jnp.concatenate(
        [spread[..., :cut].reshape(lead_shape), spread[..., cut:].reshape(lead_shape)], axis=2
    ).reshape(row_count, ROW_PARTS * seg_count * rows)
    slot_chunks, layer_out, grad_all = whole_step(
        outgoing,
        place_two,
        cotangent,
        hidden,
        hidden.T,
        rows,
        seg_count,
        (0, listed, seg_count),
    )
    grad_view = grad_all.reshape(seg_count, seg_len, ROW_PARTS, seg_count * rows)
    low, rest = seg_count * cut, rows - cut
    grad_hidden = jnp.stack(
        [
            jnp.concatenate(
                [
                    grad_view[seg, :, :, seg * cut : (seg + 1) * cut],
                    grad_view[seg, :, :, low + seg * rest : low + (seg + 1) * rest],
                ],
                axis=2,
            )
            for seg in range(seg_count)
        ]
    ).reshape(row_count, ff_local)
    own_grad = join_panels(slot_chunks, 1, rows)
    expert_grad = jnp.transpose(own_grad, (1, 0, 2)).astype(jnp.float32)
    return (layer_out, grad_hidden, expert_grad)


def solution(mesh):
    placed = (
        P("dp", "tensor"),
        P("dp", "tensor"),
        P("tensor", "dp", None),
        P("dp", None),
        P("dp", None),
        P(),
    )
    return jax.shard_map(
        body,
        mesh=mesh,
        in_specs=placed,
        out_specs=(P("dp", "tensor"), P("dp", "tensor"), P("tensor", "dp", None)),
        check_vma=False,
    )
```

```python
import functools
import jax
import jax.numpy as jnp
from jax import lax
from jax.experimental import pallas as pl
from jax.experimental.pallas import tpu as pltpu
from jax.sharding import PartitionSpec as P

K = 4
ROW_PARTS = 4
TILE_ROWS = 16


def two_pieces(values):
    high = lax.reduce_precision(values, 8, 7)
    low = lax.reduce_precision(values - high, 8, 7)
    return high, low


def split_panels(panels, count):
    lead, ff_local, width = panels.shape
    cols = count // ROW_PARTS
    rows = ff_local // ROW_PARTS
    view = panels.reshape(lead, ROW_PARTS, rows, cols, width // cols)
    return jnp.transpose(view, (1, 3, 0, 2, 4)).reshape(count, lead * rows, width // cols)


def join_panels(chunks, lead, rows):
    count, high, lanes = chunks.shape
    cols = count // ROW_PARTS
    view = chunks[:, high - lead * rows :].reshape(ROW_PARTS, cols, lead, rows, lanes)
    return jnp.transpose(view, (2, 0, 3, 1, 4)).reshape(lead, ROW_PARTS * rows, cols * lanes)


def coefficients(inner, meta_row, listed, seg_count, place_ref):
    count, padded, lanes = inner.shape
    base = (meta_row // TILE_ROWS) * TILE_ROWS
    tail = inner[:, pl.ds(base, TILE_ROWS), :].astype(jnp.float32)
    which = lax.broadcasted_iota(jnp.int32, tail.shape, 1)
    meta = jnp.sum(jnp.where(which == meta_row - base, tail, 0.0), axis=1)
    lane = lax.broadcasted_iota(jnp.int32, (count, lanes), 1).astype(jnp.float32)
    found = []
    for seg in range(seg_count):
        pieces = []
        for piece in (1, 2):
            total = jnp.zeros((count, lanes), jnp.float32)
            for k in range(K):
                at = seg * K + k
                weight = meta[:, piece * listed + at : piece * listed + at + 1]
                total = total + jnp.where(lane == meta[:, at : at + 1], weight, 0.0)
            pieces.append(total)
        rows = jnp.concatenate(pieces, axis=1).astype(jnp.bfloat16)
        found.append(jnp.dot(rows, place_ref[...], preferred_element_type=jnp.float32))
    return jnp.concatenate(found, axis=0)


def step_body(
    rows, seg_count, decode, x_ref, place_ref, cot_ref, hid_ref, hid_t_ref,
    slot_ref, layer_ref, grad_ref,
    full, in_one, in_two, in_three, held, wide_one, wide_two, out_two, out_three, out_four,
    merged, partial, *sems
):
    me, side = lax.axis_index("dp"), lax.axis_index("tensor")
    count, padded, lanes = x_ref.shape
    tall, part = cot_ref.shape
    width = full.shape[1]
    sides = lax.axis_size("tensor")
    both = seg_count * rows
    cols = count // ROW_PARTS
    pair_lanes = 2 * lanes
    barrier = pltpu.get_barrier_semaphore()

    def greet(step, carry):
        pl.semaphore_signal(
            barrier,
            inc=1,
            device_id={"dp": lax.rem(me + step, count)},
            device_id_type=pl.DeviceIdType.MESH,
        )
        return carry

    def greet_side(step, carry):
        pl.semaphore_signal(
            barrier,
            inc=1,
            device_id={"tensor": lax.rem(side + step, sides)},
            device_id_type=pl.DeviceIdType.MESH,
        )
        return carry

    lax.fori_loop(1, count, greet, 0)
    lax.fori_loop(1, sides, greet_side, 0)
    pl.semaphore_wait(barrier, count + sides - 2)

    half = padded // 2
    cut = half - (padded - rows)
    slim = ((0, half), (half, half))
    double = ((0, seg_count * cut), (seg_count * cut, seg_count * (rows - cut)))

    def copies(source, target, send_sem, recv_sem, piece, piece_index):
        def copy(step):
            swing = lax.div(step, 2) * (1 - 2 * lax.rem(step, 2))
            peer = lax.rem(me + count // 2 + swing, count)
            mark = piece_index * count + step
            return pltpu.make_async_remote_copy(
                src_ref=source.at[peer, pl.ds(*piece)],
                dst_ref=target.at[me, pl.ds(*piece)],
                send_sem=send_sem.at[mark],
                recv_sem=recv_sem.at[mark],
                device_id={"dp": peer},
                device_id_type=pl.DeviceIdType.MESH,
            )

        return copy

    def stripe(index):
        return pl.ds(pl.multiple_of(index * part, 128), part)

    def gather_copy(step):
        return pltpu.make_async_remote_copy(
            src_ref=cot_ref,
            dst_ref=full.at[:, stripe(side)],
            send_sem=sems[8].at[step],
            recv_sem=sems[9].at[step],
            device_id={"tensor": lax.rem(side + step, sides)},
            device_id_type=pl.DeviceIdType.MESH,
        )

    def scatter_copy(step):
        peer = lax.rem(side + step, sides)
        return pltpu.make_async_remote_copy(
            src_ref=partial.at[:, stripe(peer)],
            dst_ref=held.at[side],
            send_sem=sems[10].at[step],
            recv_sem=sems[11].at[step],
            device_id={"tensor": peer},
            device_id_type=pl.DeviceIdType.MESH,
        )

    def begin(copy, steps):
        def one(step, carry):
            copy(step).start()
            return carry

        lax.fori_loop(1, steps, one, 0)

    def finish(copy, steps):
        def one(step, carry):
            copy(step).wait()
            return carry

        lax.fori_loop(1, steps, one, 0)

    def spot(piece, seg, row, lead):
        if lead == 1:
            return row + padded - rows - piece * half
        return seg * (rows - cut) + row - cut if piece else seg * cut + row

    def mix(coef, piece, source, target, lead_in, lead_out):
        start_in, high_in = (double if lead_in > 1 else slim)[piece]
        start_out, high_out = (double if lead_out > 1 else slim)[piece]
        for row in range(cut if piece else 0, rows if piece else cut, 2):
            pair = jnp.concatenate(
                [
                    jnp.concatenate(
                        [
                            source[
                                pl.ds(
                                    count * start_in + spot(piece, seg, row + i, lead_in),
                                    count,
                                    stride=high_in,
                                ),
                                :,
                            ]
                            for seg in range(lead_in)
                        ],
                        axis=0,
                    )
                    for i in (0, 1)
                ],
                axis=1,
            ).astype(jnp.bfloat16)
            summed = jnp.dot(
                coef, jnp.concatenate([pair, pair], axis=0), preferred_element_type=jnp.float32
            )
            for seg in range(lead_out):
                for i in (0, 1):
                    target[
                        pl.ds(
                            count * start_out + spot(piece, seg, row + i, lead_out),
                            count,
                            stride=high_out,
                        ),
                        :,
                    ] = summed[seg * count : (seg + 1) * count, i * lanes : (i + 1) * lanes]

    def widen(source, target, piece):
        start, high = piece
        target[pl.ds(count * start, count * high), :] = (
            source[:, pl.ds(start, high), :].astype(jnp.float32).reshape(count * high, lanes)
        )

    def narrow(source, target, piece):
        start, high = piece
        target[:, pl.ds(start, high), :] = (
            source[pl.ds(count * start, count * high), :]
            .reshape(count, high, lanes)
            .astype(jnp.bfloat16)
        )

    first = [copies(x_ref, in_one, sems[0], sems[1], slim[p], p) for p in (0, 1)]
    second = [copies(out_two, in_two, sems[2], sems[3], double[p], p) for p in (0, 1)]
    third = [copies(out_three, in_three, sems[4], sems[5], double[p], p) for p in (0, 1)]
    fourth = [copies(out_four, slot_ref, sems[6], sems[7], slim[p], p) for p in (0, 1)]

    begin(first[0], count)
    begin(first[1], count)
    begin(gather_copy, sides)
    in_one[pl.ds(me, 1)] = x_ref[pl.ds(me, 1)]
    full[:, stripe(side)] = cot_ref[...]
    finish(first[0], count)
    coef = coefficients(in_one, *decode, place_ref)
    for p in (0, 1):
        if p:
            finish(first[1], count)
        widen(in_one, wide_one, slim[p])
        mix(coef.astype(jnp.bfloat16), p, wide_one, wide_two, 1, seg_count)
        narrow(wide_two, out_two, double[p])
        begin(second[p], count)
    in_two[pl.ds(me, 1)] = out_two[pl.ds(me, 1)]

    finish(gather_copy, sides)

    def seg_grads(block, carry):
        at = pl.ds(pl.multiple_of(block * pair_lanes, pair_lanes), pair_lanes)
        product = jnp.dot(hid_t_ref[...], full[:, at], preferred_element_type=jnp.float32)
        for up in range(ROW_PARTS):
            for i in (0, 1):
                out_three[pl.ds(up * cols + block * 2 + i, 1)] = product[
                    up * both : (up + 1) * both, i * lanes : (i + 1) * lanes
                ].astype(jnp.bfloat16)[None]
        return carry

    lax.fori_loop(0, width // pair_lanes, seg_grads, 0)
    begin(third[0], count)
    begin(third[1], count)
    in_three[pl.ds(me, 1)] = out_three[pl.ds(me, 1)]

    finish(second[0], count)
    finish(second[1], count)
    wide_two[...] = in_two[...].astype(jnp.float32).reshape(count * both, lanes)

    def forward(block, carry):
        at = pl.ds(pl.multiple_of(block * pair_lanes, pair_lanes), pair_lanes)
        panel = jnp.concatenate(
            [
                jnp.concatenate(
                    [
                        wide_two[
                            pl.ds(
                                pl.multiple_of((up * cols + block * 2 + i) * both, 8), both
                            ),
                            :,
                        ]
                        for up in range(ROW_PARTS)
                    ],
                    axis=0,
                )
                for i in (0, 1)
            ],
            axis=1,
        ).astype(jnp.bfloat16)
        merged[:, at] = panel
        partial[:, at] = jnp.dot(
            hid_ref[...], panel, preferred_element_type=jnp.float32
        ).astype(jnp.bfloat16)
        return carry

    lax.fori_loop(0, width // pair_lanes, forward, 0)
    begin(scatter_copy, sides)
    held[pl.ds(side, 1)] = partial[:, stripe(side)][None]

    height = 64

    def backward(block, carry):
        at = pl.ds(pl.multiple_of(block * height, height), height)
        grad_ref[at, :] = lax.dot_general(
            full[at, :],
            merged[...],
            (((1,), (1,)), ((), ())),
            preferred_element_type=jnp.float32,
        ).astype(jnp.bfloat16)
        return carry

    lax.fori_loop(0, tall // height, backward, 0)

    turned = jnp.transpose(coef)
    by_segment = jnp.concatenate([turned[:count], turned[count:]], axis=1)
    wide_one[...] = jnp.zeros_like(wide_one)
    for p in (0, 1):
        finish(third[p], count)
        widen(in_three, wide_two, double[p])
        mix(by_segment.astype(jnp.bfloat16), p, wide_two, wide_one, seg_count, 1)
        narrow(wide_one, out_four, slim[p])
        begin(fourth[p], count)
    slot_ref[pl.ds(me, 1)] = out_four[pl.ds(me, 1)]

    finish(scatter_copy, sides)

    def add_up(block, carry):
        at = pl.ds(pl.multiple_of(block * height, height), height)
        total = held[0, at, :].astype(jnp.float32)
        for other in range(1, sides):
            total = total + held[other, at, :].astype(jnp.float32)
        layer_ref[at, :] = total.astype(jnp.bfloat16)
        return carry

    lax.fori_loop(0, tall // height, add_up, 0)
    finish(fourth[0], count)
    finish(fourth[1], count)


def whole_step(blocks, place, cotangent, hidden, hidden_t, rows, seg_count, decode):
    count, padded, lanes = blocks.shape
    sides = lax.axis_size("tensor")
    tall, part = cotangent.shape
    both = seg_count * rows
    high = ROW_PARTS * both
    vmem = pl.BlockSpec(memory_space=pltpu.VMEM)
    narrow = functools.partial(pltpu.VMEM, dtype=jnp.bfloat16)
    results = tuple(
        jax.ShapeDtypeStruct(shape, jnp.bfloat16)
        for shape in ((count, padded, lanes), (tall, part), (tall, high))
    )
    return pl.pallas_call(
        functools.partial(step_body, rows, seg_count, decode),
        out_shape=results,
        in_specs=[vmem] * 5,
        out_specs=(vmem,) * 3,
        scratch_shapes=[
            narrow((tall, part * sides)),
            narrow((count, padded, lanes)),
            narrow((count, both, lanes)),
            narrow((count, both, lanes)),
            narrow((sides, tall, part)),
            pltpu.VMEM((count * padded, lanes), jnp.float32),
            pltpu.VMEM((count * both, lanes), jnp.float32),
            narrow((count, both, lanes)),
            narrow((count, both, lanes)),
            narrow((count, padded, lanes)),
            narrow((high, part * sides)),
            narrow((tall, part * sides)),
        ]
        + [pltpu.SemaphoreType.DMA((2 * count,))] * 8
        + [pltpu.SemaphoreType.DMA((sides,))] * 4,
        compiler_params=pltpu.CompilerParams(
            collective_id=0, has_side_effects=True, vmem_limit_bytes=56 * 1024 * 1024
        ),
    )(blocks, place, cotangent, hidden, hidden_t)


def body(hidden_act, cotangent, down_table, expert_ids, merge_weights, owner_slot):
    count = lax.axis_size("dp")
    seg_count = expert_ids.shape[0]
    ff_local, _, width = down_table.shape
    row_count = hidden_act.shape[0]
    seg_len = row_count // seg_count
    rows = ff_local // ROW_PARTS
    padded = -(-(rows + 1) // 8) * 8
    lanes = width * ROW_PARTS // count
    listed = seg_count * K

    high, low = two_pieces(merge_weights)
    meta = jnp.concatenate(
        [expert_ids.astype(jnp.float32).reshape(-1), high.reshape(-1), low.reshape(-1)]
    ).astype(jnp.bfloat16)
    meta = jnp.pad(meta[None, :], ((0, padded - rows - 1), (0, lanes - 3 * listed)))
    table_chunks = split_panels(jnp.transpose(down_table, (1, 0, 2)), count)
    outgoing = jnp.concatenate(
        [jnp.broadcast_to(meta, (count,) + meta.shape), table_chunks], axis=1
    )
    slot_range = jnp.arange(count, dtype=jnp.int32)
    place = jnp.pad(
        (owner_slot[:, None] == slot_range[None, :]).astype(jnp.bfloat16),
        ((0, lanes - owner_slot.shape[0]), (0, 0)),
    )
    nothing = jnp.zeros_like(place)
    place_two = jnp.concatenate(
        [
            jnp.concatenate([place, nothing], axis=1),
            jnp.concatenate([nothing, place], axis=1),
        ],
        axis=0,
    )
    cut = padded // 2 - (padded - rows)
    parts = hidden_act.reshape(seg_count, seg_len, ROW_PARTS, 1, rows)
    same = jnp.eye(seg_count, dtype=jnp.bool_)[:, None, None, :, None]
    spread = jnp.where(same, parts, 0)
    lead_shape = (row_count, ROW_PARTS, -1)
    hidden = jnp.concatenate(
        [spread[..., :cut].reshape(lead_shape), spread[..., cut:].reshape(lead_shape)], axis=2
    ).reshape(row_count, ROW_PARTS * seg_count * rows)
    slot_chunks, layer_out, grad_all = whole_step(
        outgoing,
        place_two,
        cotangent,
        hidden,
        hidden.T,
        rows,
        seg_count,
        (0, listed, seg_count),
    )
    grad_view = grad_all.reshape(seg_count, seg_len, ROW_PARTS, seg_count * rows)
    low, rest = seg_count * cut, rows - cut
    grad_hidden = jnp.stack(
        [
            jnp.concatenate(
                [
                    grad_view[seg, :, :, seg * cut : (seg + 1) * cut],
                    grad_view[seg, :, :, low + seg * rest : low + (seg + 1) * rest],
                ],
                axis=2,
            )
            for seg in range(seg_count)
        ]
    ).reshape(row_count, ff_local)
    own_grad = join_panels(slot_chunks, 1, rows)
    expert_grad = jnp.transpose(own_grad, (1, 0, 2)).astype(jnp.float32)
    return (layer_out, grad_hidden, expert_grad)


def solution(mesh):
    placed = (
        P("dp", "tensor"),
        P("dp", "tensor"),
        P("tensor", "dp", None),
        P("dp", None),
        P("dp", None),
        P(),
    )
    return jax.shard_map(
        body,
        mesh=mesh,
        in_specs=placed,
        out_specs=(P("dp", "tensor"), P("dp", "tensor"), P("tensor", "dp", None)),
        check_vma=False,
    )
```
